32 devices in a mesh: run: 8 (over z, y), rep: 4 (over x, core).
Axes of the slice: x: 2, y: 2, z: 4, core: 2. Of those that a mesh axis runs over, the one named last changes fastest.
Arguments:
- edge_feats: bfloat16 [4, 16384, 1280], P('rep', 'run'), may hold values from -6 to 6
- edge_grads: bfloat16 [4, 16384, 640], P('rep', 'run'), may hold values from -0.059814453 to 0.059814453
- edge_system: int32 [4, 16384], P('rep', 'run'), may hold values from 0 to 5, as said below
- edge_count: int32 [4, 8], P('rep', 'run'), may hold values from 1025 to 2048
- coef: float32 [4, 6, 32], P('rep'), may hold values from 0.05 to 1
- weights: float32 [32, 1280, 640], P('rep', 'run'), may hold values from -0.15625 to 0.15625
- first_moment: float32 [32, 1280, 640], P('rep', 'run'), may hold values from -6 to 6
- second_moment: float32 [32, 1280, 640], P('rep', 'run'), may hold values from 1 to 10
Outputs:
- new_weights: float32 [32, 1280, 640], P('rep', 'run')
- new_first: float32 [32, 1280, 640], P('rep', 'run')
- new_second: float32 [32, 1280, 640], P('rep', 'run')
- merged_next: bfloat16 [4, 6, 1280, 640], P('rep', None, 'run')
The draws below stay inside these ranges and needn't reach their ends.
Inputs may be any that keep to these rules, and one draw needn't show every extreme that they name: `edge_system`: along each replica's rows the system never falls; every system number appears; the live rows of one device belong to one or two systems, two on some device in every draw.
All inputs are finite; a program needn't handle non-finite values.
Results may differ from the reference program's by a relative error of at most 0.001.
The reference program's roundings to bfloat16 on the way (of `rounded`) count: a program that leaves them out, or rounds other values in their place, can miss the bound.
Values may be sent and summed in bfloat16 or wider, within the bound.
A program may use at most 128 MiB of HBM per device.

```python
import math
import jax
import jax.numpy as jnp
from jax import lax

DIN = 1280
DOUT = 640
EXPERTS = 32
NSYS = 6
ROWS = 2048
EDGES = 16384
N_RUN = 8
N_REP = 4


def draw_edge_system(key, part):

    def replica_ids(replica_key):
        key_block, key_offset = jax.random.split(replica_key)
        blocks = jnp.sort(jax.random.randint(key_block, (NSYS - 1,), 0, N_RUN - NSYS + 1))
        offsets = jnp.sort(jax.random.randint(key_offset, (NSYS - 1,), 1, ROWS // 2 + 1))
        bounds = (jnp.arange(1, NSYS) + blocks) * ROWS + offsets
        position = jnp.arange(N_RUN * ROWS)
        return jnp.sum((position[:, None] >= bounds[None, :]).astype(jnp.int32), axis=1).astype(jnp.int32)
    replica_keys = jax.random.split(key, N_REP)
    return jax.vmap(replica_ids)(replica_keys)


def place_ends(values, rng, smallest, top_value):
    dims = values.shape
    place = [jax.random.randint(jax.random.fold_in(rng, axis), (), 0, dims[axis]) for axis in range(len(dims))]
    values = values.at[tuple(place)].set(smallest)
    longest = dims.index(max(dims))
    place[longest] = (place[longest] + 1) % dims[longest]
    return values.at[tuple(place)].set(top_value)


def block_scale(stream_key, shape, shards, low, high):
    level, own = 1.0, jax.random.fold_in(stream_key, 6)
    for axis_at, shards_of in shards:
        draws = jnp.exp(jax.random.uniform(jax.random.fold_in(own, axis_at), (shards_of,), jnp.float32, low / len(shards), high / len(shards)))
        level = level * jnp.repeat(draws, shape[axis_at] // shards_of).reshape([-1 if axis == axis_at else 1 for axis in range(len(shape))])
    return level


def scatter_about(rng, extent, scale, reach, cuts=(), dtype=jnp.bfloat16):
    result = jax.random.normal(rng, extent, jnp.float32) * scale
    if len(cuts) > 0:
        result = block_scale(rng, extent, cuts, -0.22, 0.18) * result
    return jnp.clip(result, min=-reach, max=reach).astype(dtype)


def setup_inputs(seed: int = 0) -> dict:
    keys = jax.random.split(jax.random.key(seed), 9)
    edge_feats = scatter_about(keys[0], (N_REP, EDGES, DIN), 1.0, 6.0, ((0, 4), (1, 8)))
    edge_grads = scatter_about(keys[1], (N_REP, EDGES, DOUT), 0.01, 0.059814453, ((0, 4), (1, 8)))
    edge_system = draw_edge_system(jax.random.fold_in(keys[8], 71), 0)
    edge_count = place_ends(jax.random.randint(keys[3], (N_REP, N_RUN), ROWS // 2 + 1, ROWS + 1), jax.random.fold_in(keys[3], 1), ROWS // 2 + 1, ROWS).astype(jnp.int32)
    coef = jnp.clip(jnp.exp(math.log(1.0) - 2.9957323 * jax.random.uniform(keys[4], (N_REP, NSYS, EXPERTS), jnp.float32) ** block_scale(keys[4], (N_REP, NSYS, EXPERTS), ((0, 4),), -0.2, 0.2)), 0.05, 1.0)
    weights = scatter_about(keys[5], (EXPERTS, DIN, DOUT), DIN ** -0.5, 0.15625, ((0, 4), (1, 8)), jnp.float32)
    first_moment = scatter_about(keys[6], (EXPERTS, DIN, DOUT), 1.0, 6.0, ((0, 4), (1, 8)), jnp.float32)
    second_moment = jnp.clip(jnp.exp(math.log(10.0) - 2.3025851 * jax.random.uniform(keys[7], (EXPERTS, DIN, DOUT), jnp.float32) ** block_scale(keys[7], (EXPERTS, DIN, DOUT), ((0, 4), (1, 8)), -0.2, 0.2)), 1.0, 10.0)
    return {"edge_feats": edge_feats, "edge_grads": edge_grads, "edge_system": edge_system, "edge_count": edge_count, "coef": coef, "weights": weights, "first_moment": first_moment, "second_moment": second_moment}


def system_sums(feats, grads, system, counts):
    feat_blocks = feats.reshape(N_RUN, ROWS, DIN)
    grad_blocks = grads.reshape(N_RUN, ROWS, DOUT)
    sys_blocks = system.reshape(N_RUN, ROWS)

    def device_step(total, item):
        feat_rows, grad_rows, sys_rows, live_count = item
        live = jnp.arange(ROWS) < live_count
        first = sys_rows[0]
        last = lax.dynamic_index_in_dim(sys_rows, live_count - 1, 0, keepdims=False)
        left = feat_rows.astype(jnp.float32)

        def slot(offset):
            keep = live & (sys_rows == first + offset)
            right = jnp.where(keep[:, None], grad_rows.astype(jnp.float32), jnp.float32(0.0))
            return lax.dot_general(left, right, (((0,), (0,)), ((), ())), precision=lax.Precision.HIGHEST)
        lower = slot(0)
        upper = lax.cond(last > first, lambda: slot(1), lambda: jnp.zeros_like(lower))
        total = total.at[first].add(lower)
        total = total.at[jnp.minimum(first + 1, NSYS - 1)].add(upper)
        return (total, None)
    start = jnp.zeros((NSYS, DIN, DOUT), jnp.float32)
    total, _ = lax.scan(device_step, start, (feat_blocks, grad_blocks, sys_blocks, counts))
    return total

def reference(edge_feats, edge_grads, edge_system, edge_count, coef, weights, first_moment, second_moment):

    def replica_step(total, item):
        feats, grads, system, counts, group_coef = item
        sums = system_sums(feats, grads, system, counts)
        mixed = jnp.einsum('se,sio->eio', group_coef, sums, precision=lax.Precision.HIGHEST)
        return (total + mixed, None)
    start = jnp.zeros((EXPERTS, DIN, DOUT), jnp.float32)
    expert_grad, _ = lax.scan(replica_step, start, (edge_feats, edge_grads, edge_system, edge_count, coef))
    new_first = 0.9 * first_moment + 0.1 * expert_grad
    new_second = 0.999 * second_moment + 0.001 * expert_grad * expert_grad
    corr_first = 1.0 - 0.9 ** 10
    corr_second = 1.0 - 0.999 ** 10
    new_weights = weights - 0.01 * (new_first / corr_first) / (jnp.sqrt(new_second / corr_second) + 1e-08)
    rounded = lax.optimization_barrier(new_weights.astype(jnp.bfloat16))
    flat = rounded.astype(jnp.float32).reshape(EXPERTS, DIN * DOUT)
    merged = jnp.einsum('rse,ek->rsk', coef, flat, precision=lax.Precision.HIGHEST)
    merged_next = merged.reshape(N_REP, NSYS, DIN, DOUT).astype(jnp.bfloat16)
    return (new_weights, new_first, new_second, merged_next)
```

```python
import jax
import jax.numpy as jnp
from jax import lax
from jax.sharding import PartitionSpec as P


def on_device(
    edge_feats, edge_grads, edge_system, edge_count, coef, weights, first_moment, second_moment
):
    feats = edge_feats[0]
    grads = edge_grads[0]
    system = edge_system[0]
    live_count = edge_count[0, 0]
    group_coef = coef[0]
    nsys = group_coef.shape[0]
    rows = system.shape[0]
    live = jnp.arange(rows) < live_count
    first = system[0]
    empty = jnp.zeros_like(grads)
    lower = jnp.where((live & (system == first))[:, None], grads, empty)
    upper = jnp.where((live & (system == first + 1))[:, None], grads, empty)
    right = jnp.concatenate([lower, upper], axis=1)
    slots = lax.dot_general(
        feats, right, (((0,), (0,)), ((), ())), preferred_element_type=jnp.float32
    ).astype(jnp.bfloat16)
    pieces = lax.all_to_all(slots, "run", split_axis=0, concat_axis=0, tiled=True)
    firsts = lax.all_gather(first, "run")
    n_run = firsts.shape[0]
    pieces = pieces.reshape(n_run, -1, pieces.shape[1])
    dout = grads.shape[1]
    sums = []
    for s in range(nsys):
        total = 0.0
        for k in range(n_run):
            low = pieces[k, :, :dout].astype(jnp.float32)
            high = pieces[k, :, dout:].astype(jnp.float32)
            total = total + jnp.where(firsts[k] == s, low, 0.0)
            total = total + jnp.where(firsts[k] + 1 == s, high, 0.0)
        sums.append(total.astype(jnp.bfloat16))
    every_sum = lax.all_gather(jnp.stack(sums), "rep", axis=0, tiled=True)
    every_coef = lax.all_gather(group_coef, "rep", axis=0, tiled=True)
    held = weights.shape[0]
    own_coef = lax.dynamic_slice_in_dim(every_coef, lax.axis_index("rep") * held, held, 1)
    expert_grad = jnp.einsum(
        "ge,gio->eio", own_coef, every_sum.astype(jnp.float32), precision=lax.Precision.HIGHEST
    )
    new_first = 0.9 * first_moment + 0.1 * expert_grad
    new_second = 0.999 * second_moment + 0.001 * expert_grad * expert_grad
    corr_first = 1.0 - 0.9**10
    corr_second = 1.0 - 0.999**10
    new_weights = weights - 0.01 * (new_first / corr_first) / (
        jnp.sqrt(new_second / corr_second) + 1e-08
    )
    rounded = lax.optimization_barrier(new_weights.astype(jnp.bfloat16))
    every_expert = lax.all_gather(rounded, "rep", axis=0, tiled=True)
    experts, din_local, dout = every_expert.shape
    flat = every_expert.astype(jnp.float32).reshape(experts, din_local * dout)
    merged = jnp.dot(group_coef, flat, precision=lax.Precision.HIGHEST)
    merged_next = merged.reshape(nsys, din_local, dout).astype(jnp.bfloat16)
    return (new_weights, new_first, new_second, merged_next[None])


def solution(mesh):
    placed = (
        P("rep", "run", None),
        P("rep", "run", None),
        P("rep", "run"),
        P("rep", "run"),
        P("rep", None, None),
        P("rep", "run", None),
        P("rep", "run", None),
        P("rep", "run", None),
    )
    return jax.shard_map(
        on_device,
        mesh=mesh,
        in_specs=placed,
        out_specs=(
            P("rep", "run", None),
            P("rep", "run", None),
            P("rep", "run", None),
            P("rep", None, "run", None),
        ),
        check_vma=False,
    )
```

```python
import functools
import jax
import jax.numpy as jnp
from jax import lax
from jax.experimental import pallas as pl
from jax.experimental.pallas import tpu as pltpu
from jax.sharding import PartitionSpec as P

MESH = pl.DeviceIdType.MESH
LANES = 128


def step_kernel(
    n_run, n_rep, nsys, held, chunks, chunk_rows, dout,
    slots, meta, coef_out, merge_coef, weights, moment1, moment2,
    weights_out, moment1_out, moment2_out, merged_out,
    land, meta_land, coef_land, sums, rounded, wbuf, fbuf, sbuf, mbuf,
    a2a_send, a2a_recv, meta_send, meta_recv, coef_send, coef_recv,
    x_send, x_recv, pair_send, pair_recv, own_sem, in_sem, out_sem,
):
    me = lax.axis_index("run")
    rep = lax.axis_index("rep")
    partner = rep + 1 - 2 * lax.rem(rep, 2)
    n_x = n_rep // 2
    experts = n_rep * held

    loads = [
        pltpu.make_async_copy(src, dst, in_sem.at[i])
        for i, (src, dst) in enumerate(((weights, wbuf), (moment1, fbuf), (moment2, sbuf)))
    ]
    for load in loads:
        load.start()
    own = pltpu.make_async_copy(slots.at[me], land.at[me], own_sem)
    own.start()

    barrier = pltpu.get_barrier_semaphore()
    for o in range(1, n_run):
        pl.semaphore_signal(
            barrier, inc=1, device_id={"run": lax.rem(me + o, n_run)}, device_id_type=MESH
        )
    for o in range(1, n_rep):
        pl.semaphore_signal(
            barrier, inc=1, device_id={"rep": lax.rem(rep + o, n_rep)}, device_id_type=MESH
        )
    pl.semaphore_wait(barrier, n_run + n_rep - 2)

    started = []

    def send(src, dst, send_sem, recv_sem, device):
        copy = pltpu.make_async_remote_copy(
            src_ref=src, dst_ref=dst, send_sem=send_sem, recv_sem=recv_sem,
            device_id=device, device_id_type=MESH,
        )
        copy.start()
        started.append(copy)
        return copy

    metas = [
        send(meta, meta_land.at[me], meta_send.at[o - 1], meta_recv.at[o - 1],
             {"run": lax.rem(me + o, n_run)})
        for o in range(1, n_run)
    ]
    coefs = []
    for o in range(1, n_rep):
        dest = lax.rem(rep + o, n_rep)
        coefs.append(
            send(coef_out.at[dest], coef_land.at[rep], coef_send.at[o - 1], coef_recv.at[o - 1],
                 {"rep": dest})
        )
    pieces = []
    for c in range(chunks):
        pieces.append([])
        for o in range(1, n_run):
            dest = lax.rem(me + o, n_run)
            pieces[c].append(
                send(slots.at[dest, c], land.at[me, c], a2a_send.at[c, o - 1],
                     a2a_recv.at[c, o - 1], {"run": dest})
            )

    meta_land[me] = meta[...]
    coef_land[rep] = coef_out[rep]
    own.wait()
    for copy in metas:
        copy.wait_recv()
    for copy in coefs:
        copy.wait_recv()
    for load in loads:
        load.wait()

    group = 16 if chunk_rows % 16 == 0 else chunk_rows
    lane_steps = dout // LANES

    def tiles(body):
        def step(i, carry):
            row = lax.div(i, lane_steps) * group
            lane = lax.rem(i, lane_steps) * LANES
            body(pl.multiple_of(row, group), pl.multiple_of(lane, LANES))
            return carry

        lax.fori_loop(0, (chunk_rows // group) * lane_steps, step, 0)

    def spread(buf, kind, c):
        direct = send(buf.at[c, rep], buf.at[c, rep], pair_send.at[kind, c, 0],
                      pair_recv.at[kind, c, 0], {"rep": partner})
        across = [
            send(buf.at[c, rep], buf.at[c, rep], x_send.at[kind, c, j - 1],
                 x_recv.at[kind, c, j - 1], {"rep": lax.rem(rep + 2 * j, n_rep)})
            for j in range(1, n_x)
        ]
        return direct, across

    def collect(buf, kind, c, direct, across):
        relays = []
        for j in range(1, n_x):
            across[j - 1].wait_recv()
            slot = lax.rem(rep + n_rep - 2 * j, n_rep)
            relays.append(
                send(buf.at[c, slot], buf.at[c, slot], pair_send.at[kind, c, j],
                     pair_recv.at[kind, c, j], {"rep": partner})
            )
        direct.wait_recv()
        for relay in relays:
            relay.wait_recv()

    def sum_systems(c):
        def body(row, lane):
            rows = pl.ds(row, group)
            total = [jnp.zeros((group, LANES), jnp.float32)] * nsys
            for k in range(n_run):
                low = land[k, c, rows, pl.ds(lane, LANES)].astype(jnp.float32)
                high = land[k, c, rows, pl.ds(lane + dout, LANES)].astype(jnp.float32)
                for s in range(nsys):
                    total[s] = (
                        total[s]
                        + meta_land[k, s + 1 : s + 2, :] * low
                        + meta_land[k, s : s + 1, :] * high
                    )
            for s in range(nsys):
                sums[c, rep, s, rows, pl.ds(lane, LANES)] = total[s].astype(jnp.bfloat16)

        tiles(body)

    def update(c):
        def body(row, lane):
            rows, lanes = pl.ds(row, group), pl.ds(lane, LANES)
            place = pl.ds(c * chunk_rows + row, group)
            grad = [jnp.zeros((group, LANES), jnp.float32)] * held
            for r in range(n_rep):
                for s in range(nsys):
                    part = sums[c, r, s, rows, lanes].astype(jnp.float32)
                    for e in range(held):
                        at = s * held + e
                        grad[e] = grad[e] + coef_land[r, at : at + 1, :] * part
            for e in range(held):
                new_first = 0.9 * fbuf[e, place, lanes] + 0.1 * grad[e]
                new_second = 0.999 * sbuf[e, place, lanes] + 0.001 * grad[e] * grad[e]
                corr_first = 1.0 - 0.9**10
                corr_second = 1.0 - 0.999**10
                new_weights = wbuf[e, place, lanes] - 0.01 * (new_first / corr_first) / (
                    jnp.sqrt(new_second / corr_second) + 1e-08
                )
                fbuf[e, place, lanes] = new_first
                sbuf[e, place, lanes] = new_second
                wbuf[e, place, lanes] = new_weights
                rounded[c, rep, e, rows, lanes] = new_weights.astype(jnp.bfloat16)

        tiles(body)

    def merge(c):
        def body(row, lane):
            rows, lanes = pl.ds(row, group), pl.ds(lane, LANES)
            total = [jnp.zeros((group, LANES), jnp.float32)] * nsys
            for r in range(n_rep):
                for e in range(held):
                    part = rounded[c, r, e, rows, lanes].astype(jnp.float32)
                    for s in range(nsys):
                        at = s * experts + r * held + e
                        total[s] = total[s] + merge_coef[at : at + 1, :] * part
            for s in range(nsys):
                mbuf[c, s, rows, lanes] = total[s].astype(jnp.bfloat16)

        tiles(body)

    stores = []

    def store(src, dst, kind, c):
        copy = pltpu.make_async_copy(src, dst, out_sem.at[kind, c])
        copy.start()
        stores.append(copy)

    def finish(c, moving):
        collect(rounded, 1, c, *moving)
        merge(c)
        store(mbuf.at[c], merged_out.at[:, pl.ds(c * chunk_rows, chunk_rows), :], 3, c)

    waiting = None
    for c in range(chunks):
        for copy in pieces[c]:
            copy.wait_recv()
        sum_systems(c)
        moving = spread(sums, 0, c)
        if waiting is not None:
            finish(c - 1, waiting)
        collect(sums, 0, c, *moving)
        update(c)
        waiting = spread(rounded, 1, c)
        place = pl.ds(c * chunk_rows, chunk_rows)
        store(wbuf.at[:, place, :], weights_out.at[:, place, :], 0, c)
        store(fbuf.at[:, place, :], moment1_out.at[:, place, :], 1, c)
        store(sbuf.at[:, place, :], moment2_out.at[:, place, :], 2, c)
    finish(chunks - 1, waiting)
    for copy in started:
        copy.wait_send()
    for copy in stores:
        copy.wait()


def on_device(
    n_run, n_rep,
    edge_feats, edge_grads, edge_system, edge_count, coef, weights, first_moment, second_moment
):
    feats = edge_feats[0]
    grads = edge_grads[0]
    system = edge_system[0]
    live_count = edge_count[0, 0]
    group_coef = coef[0]
    nsys, experts = group_coef.shape
    held, din_local, dout = weights.shape
    live = jnp.arange(system.shape[0]) < live_count
    first = system[0]
    empty = jnp.zeros_like(grads)
    lower = jnp.where((live & (system == first))[:, None], grads, empty)
    upper = jnp.where((live & (system == first + 1))[:, None], grads, empty)
    right = jnp.concatenate([lower, upper], axis=1)
    slots = lax.dot_general(
        feats, right, (((0,), (0,)), ((), ())), preferred_element_type=jnp.float32
    ).astype(jnp.bfloat16)

    chunk_rows = 32 if din_local % 32 == 0 else din_local
    chunks = din_local // chunk_rows
    slots = slots.reshape(n_run, chunks, chunk_rows, 2 * dout)
    meta_rows = -(-(nsys + 1) // 8) * 8
    marks = (jnp.arange(meta_rows) == first + 1).astype(jnp.float32)
    meta = jnp.broadcast_to(marks[:, None], (meta_rows, LANES))
    by_owner = group_coef.reshape(nsys, n_rep, held).transpose(1, 0, 2).reshape(n_rep, nsys * held)
    coef_out = jnp.broadcast_to(by_owner[:, :, None], (n_rep, nsys * held, LANES))
    merge_coef = jnp.broadcast_to(
        group_coef.reshape(nsys * experts)[:, None], (nsys * experts, LANES)
    )

    bf16, f32 = jnp.bfloat16, jnp.float32
    dma = pltpu.SemaphoreType.DMA
    n_x = n_rep // 2
    anywhere = pl.BlockSpec(memory_space=pl.ANY)
    vmem = pl.BlockSpec(memory_space=pltpu.VMEM)
    block = jax.ShapeDtypeStruct(weights.shape, f32)
    outs = pl.pallas_call(
        functools.partial(step_kernel, n_run, n_rep, nsys, held, chunks, chunk_rows, dout),
        out_shape=(block, block, block, jax.ShapeDtypeStruct((nsys, din_local, dout), bf16)),
        in_specs=[anywhere, vmem, vmem, vmem, anywhere, anywhere, anywhere],
        out_specs=(anywhere,) * 4,
        scratch_shapes=[
            pltpu.VMEM(slots.shape, bf16),
            pltpu.VMEM((n_run, meta_rows, LANES), f32),
            pltpu.VMEM(coef_out.shape, f32),
            pltpu.VMEM((chunks, n_rep, nsys, chunk_rows, dout), bf16),
            pltpu.VMEM((chunks, n_rep, held, chunk_rows, dout), bf16),
            pltpu.VMEM(weights.shape, f32),
            pltpu.VMEM(weights.shape, f32),
            pltpu.VMEM(weights.shape, f32),
            pltpu.VMEM((chunks, nsys, chunk_rows, dout), bf16),
            dma((chunks, n_run - 1)),
            dma((chunks, n_run - 1)),
            dma((n_run - 1,)),
            dma((n_run - 1,)),
            dma((n_rep - 1,)),
            dma((n_rep - 1,)),
            dma((2, chunks, n_x)),
            dma((2, chunks, n_x)),
            dma((2, chunks, n_x)),
            dma((2, chunks, n_x)),
            dma,
            dma((3,)),
            dma((4, chunks)),
        ],
        compiler_params=pltpu.CompilerParams(
            collective_id=0, has_side_effects=True, vmem_limit_bytes=56 * 1024 * 1024
        ),
        name="exchange_step",
    )(slots, meta, coef_out, merge_coef, weights, first_moment, second_moment)
    return (*outs[:3], outs[3][None])


def solution(mesh):
    placed = (
        P("rep", "run", None),
        P("rep", "run", None),
        P("rep", "run"),
        P("rep", "run"),
        P("rep", None, None),
        P("rep", "run", None),
        P("rep", "run", None),
        P("rep", "run", None),
    )
    return jax.shard_map(
        functools.partial(on_device, mesh.shape["run"], mesh.shape["rep"]),
        mesh=mesh,
        in_specs=placed,
        out_specs=(
            P("rep", "run", None),
            P("rep", "run", None),
            P("rep", "run", None),
            P("rep", None, "run", None),
        ),
        check_vma=False,
    )
```

```python
import functools
import jax
import jax.numpy as jnp
from jax import lax
from jax.experimental import pallas as pl
from jax.experimental.pallas import tpu as pltpu
from jax.sharding import PartitionSpec as P

MESH = pl.DeviceIdType.MESH
LANES = 128


def step_kernel(
    n_run, n_rep, nsys, held, chunks, chunk_rows, dout,
    slots, meta, coef_out, merge_coef, weights, moment1, moment2,
    weights_out, moment1_out, moment2_out, merged_out,
    land, meta_land, coef_land, sums, rounded, wbuf, fbuf, sbuf, mbuf,
    a2a_send, a2a_recv, meta_send, meta_recv, coef_send, coef_recv,
    x_send, x_recv, pair_send, pair_recv, own_sem, in_sem, out_sem,
):
    me = lax.axis_index("run")
    rep = lax.axis_index("rep")
    partner = rep + 1 - 2 * lax.rem(rep, 2)
    n_x = n_rep // 2
    experts = n_rep * held

    loads = [
        pltpu.make_async_copy(src, dst, in_sem.at[i])
        for i, (src, dst) in enumerate(((weights, wbuf), (moment1, fbuf), (moment2, sbuf)))
    ]
    for load in loads:
        load.start()
    own = pltpu.make_async_copy(slots.at[me], land.at[me], own_sem)
    own.start()

    barrier = pltpu.get_barrier_semaphore()
    for o in range(1, n_run):
        pl.semaphore_signal(
            barrier, inc=1, device_id={"run": lax.rem(me + o, n_run)}, device_id_type=MESH
        )
    for o in range(1, n_rep):
        pl.semaphore_signal(
            barrier, inc=1, device_id={"rep": lax.rem(rep + o, n_rep)}, device_id_type=MESH
        )
    pl.semaphore_wait(barrier, n_run + n_rep - 2)

    started = []

    def send(src, dst, send_sem, recv_sem, device):
        copy = pltpu.make_async_remote_copy(
            src_ref=src, dst_ref=dst, send_sem=send_sem, recv_sem=recv_sem,
            device_id=device, device_id_type=MESH,
        )
        copy.start()
        started.append(copy)
        return copy

    metas = [
        send(meta, meta_land.at[me], meta_send.at[o - 1], meta_recv.at[o - 1],
             {"run": lax.rem(me + o, n_run)})
        for o in range(1, n_run)
    ]
    coefs = []
    for o in range(1, n_rep):
        dest = lax.rem(rep + o, n_rep)
        coefs.append(
            send(coef_out.at[dest], coef_land.at[rep], coef_send.at[o - 1], coef_recv.at[o - 1],
                 {"rep": dest})
        )
    pieces = []

    def scatter(c):
        if c >= chunks:
            return
        pieces.append([])
        for o in range(1, n_run):
            dest = jnp.bitwise_xor(me, o)
            pieces[c].append(
                send(slots.at[dest, c], land.at[me, c], a2a_send.at[c, o - 1],
                     a2a_recv.at[c, o - 1], {"run": dest})
            )

    ahead = 1
    for c in range(ahead):
        scatter(c)

    meta_land[me] = meta[...]
    coef_land[rep] = coef_out[rep]
    own.wait()
    for copy in metas:
        copy.wait_recv()
    for copy in coefs:
        copy.wait_recv()
    for load in loads:
        load.wait()

    group = 16 if chunk_rows % 16 == 0 else chunk_rows
    lane_steps = dout // LANES

    def tiles(body):
        def step(i, carry):
            row = lax.div(i, lane_steps) * group
            lane = lax.rem(i, lane_steps) * LANES
            body(pl.multiple_of(row, group), pl.multiple_of(lane, LANES))
            return carry

        lax.fori_loop(0, (chunk_rows // group) * lane_steps, step, 0)

    def spread(buf, kind, c):
        direct = send(buf.at[c, rep], buf.at[c, rep], pair_send.at[kind, c, 0],
                      pair_recv.at[kind, c, 0], {"rep": partner})
        across = [
            send(buf.at[c, rep], buf.at[c, rep], x_send.at[kind, c, j - 1],
                 x_recv.at[kind, c, j - 1], {"rep": lax.rem(rep + 2 * j, n_rep)})
            for j in range(1, n_x)
        ]
        return direct, across

    def collect(buf, kind, c, direct, across):
        relays = []
        for j in range(1, n_x):
            across[j - 1].wait_recv()
            slot = lax.rem(rep + n_rep - 2 * j, n_rep)
            relays.append(
                send(buf.at[c, slot], buf.at[c, slot], pair_send.at[kind, c, j],
                     pair_recv.at[kind, c, j], {"rep": partner})
            )
        direct.wait_recv()
        for relay in relays:
            relay.wait_recv()

    def sum_systems(c):
        def body(row, lane):
            rows = pl.ds(row, group)
            total = [jnp.zeros((group, LANES), jnp.float32)] * nsys
            for k in range(n_run):
                low = land[k, c, rows, pl.ds(lane, LANES)].astype(jnp.float32)
                high = land[k, c, rows, pl.ds(lane + dout, LANES)].astype(jnp.float32)
                for s in range(nsys):
                    total[s] = (
                        total[s]
                        + meta_land[k, s + 1 : s + 2, :] * low
                        + meta_land[k, s : s + 1, :] * high
                    )
            for s in range(nsys):
                sums[c, rep, s, rows, pl.ds(lane, LANES)] = total[s].astype(jnp.bfloat16)

        tiles(body)

    def update(c):
        def body(row, lane):
            rows, lanes = pl.ds(row, group), pl.ds(lane, LANES)
            place = pl.ds(c * chunk_rows + row, group)
            grad = [jnp.zeros((group, LANES), jnp.float32)] * held
            for r in range(n_rep):
                for s in range(nsys):
                    part = sums[c, r, s, rows, lanes].astype(jnp.float32)
                    for e in range(held):
                        at = s * held + e
                        grad[e] = grad[e] + coef_land[r, at : at + 1, :] * part
            for e in range(held):
                new_first = 0.9 * fbuf[e, place, lanes] + 0.1 * grad[e]
                new_second = 0.999 * sbuf[e, place, lanes] + 0.001 * grad[e] * grad[e]
                corr_first = 1.0 - 0.9**10
                corr_second = 1.0 - 0.999**10
                new_weights = wbuf[e, place, lanes] - 0.01 * (new_first / corr_first) / (
                    jnp.sqrt(new_second / corr_second) + 1e-08
                )
                fbuf[e, place, lanes] = new_first
                sbuf[e, place, lanes] = new_second
                wbuf[e, place, lanes] = new_weights
                rounded[c, rep, e, rows, lanes] = new_weights.astype(jnp.bfloat16)

        tiles(body)

    def merge(c):
        def body(row, lane):
            rows, lanes = pl.ds(row, group), pl.ds(lane, LANES)
            total = [jnp.zeros((group, LANES), jnp.float32)] * nsys
            for r in range(n_rep):
                for e in range(held):
                    part = rounded[c, r, e, rows, lanes].astype(jnp.float32)
                    for s in range(nsys):
                        at = s * experts + r * held + e
                        total[s] = total[s] + merge_coef[at : at + 1, :] * part
            for s in range(nsys):
                mbuf[c, s, rows, lanes] = total[s].astype(jnp.bfloat16)

        tiles(body)

    stores = []

    def store(src, dst, kind, c):
        copy = pltpu.make_async_copy(src, dst, out_sem.at[kind, c])
        copy.start()
        stores.append(copy)

    def finish(c, moving):
        collect(rounded, 1, c, *moving)
        merge(c)
        store(mbuf.at[c], merged_out.at[:, pl.ds(c * chunk_rows, chunk_rows), :], 3, c)

    waiting = None
    for c in range(chunks):
        for copy in pieces[c]:
            copy.wait_recv()
        sum_systems(c)
        moving = spread(sums, 0, c)
        scatter(c + ahead)
        if waiting is not None:
            finish(c - 1, waiting)
        collect(sums, 0, c, *moving)
        update(c)
        waiting = spread(rounded, 1, c)
        place = pl.ds(c * chunk_rows, chunk_rows)
        store(wbuf.at[:, place, :], weights_out.at[:, place, :], 0, c)
        store(fbuf.at[:, place, :], moment1_out.at[:, place, :], 1, c)
        store(sbuf.at[:, place, :], moment2_out.at[:, place, :], 2, c)
    finish(chunks - 1, waiting)
    for copy in started:
        copy.wait_send()
    for copy in stores:
        copy.wait()


def on_device(
    n_run, n_rep,
    edge_feats, edge_grads, edge_system, edge_count, coef, weights, first_moment, second_moment
):
    feats = edge_feats[0]
    grads = edge_grads[0]
    system = edge_system[0]
    live_count = edge_count[0, 0]
    group_coef = coef[0]
    nsys, experts = group_coef.shape
    held, din_local, dout = weights.shape
    live = jnp.arange(system.shape[0]) < live_count
    first = system[0]
    empty = jnp.zeros_like(grads)
    lower = jnp.where((live & (system == first))[:, None], grads, empty)
    upper = jnp.where((live & (system == first + 1))[:, None], grads, empty)
    right = jnp.concatenate([lower, upper], axis=1)
    slots = lax.dot_general(
        feats, right, (((0,), (0,)), ((), ())), preferred_element_type=jnp.float32
    ).astype(jnp.bfloat16)

    chunk_rows = 32 if din_local % 32 == 0 else din_local
    chunks = din_local // chunk_rows
    slots = slots.reshape(n_run, chunks, chunk_rows, 2 * dout)
    meta_rows = -(-(nsys + 1) // 8) * 8
    marks = (jnp.arange(meta_rows) == first + 1).astype(jnp.float32)
    meta = jnp.broadcast_to(marks[:, None], (meta_rows, LANES))
    by_owner = group_coef.reshape(nsys, n_rep, held).transpose(1, 0, 2).reshape(n_rep, nsys * held)
    coef_out = jnp.broadcast_to(by_owner[:, :, None], (n_rep, nsys * held, LANES))
    merge_coef = jnp.broadcast_to(
        group_coef.reshape(nsys * experts)[:, None], (nsys * experts, LANES)
    )

    bf16, f32 = jnp.bfloat16, jnp.float32
    dma = pltpu.SemaphoreType.DMA
    n_x = n_rep // 2
    anywhere = pl.BlockSpec(memory_space=pl.ANY)
    vmem = pl.BlockSpec(memory_space=pltpu.VMEM)
    block = jax.ShapeDtypeStruct(weights.shape, f32)
    outs = pl.pallas_call(
        functools.partial(step_kernel, n_run, n_rep, nsys, held, chunks, chunk_rows, dout),
        out_shape=(block, block, block, jax.ShapeDtypeStruct((nsys, din_local, dout), bf16)),
        in_specs=[anywhere, vmem, vmem, vmem, anywhere, anywhere, anywhere],
        out_specs=(anywhere,) * 4,
        scratch_shapes=[
            pltpu.VMEM(slots.shape, bf16),
            pltpu.VMEM((n_run, meta_rows, LANES), f32),
            pltpu.VMEM(coef_out.shape, f32),
            pltpu.VMEM((chunks, n_rep, nsys, chunk_rows, dout), bf16),
            pltpu.VMEM((chunks, n_rep, held, chunk_rows, dout), bf16),
            pltpu.VMEM(weights.shape, f32),
            pltpu.VMEM(weights.shape, f32),
            pltpu.VMEM(weights.shape, f32),
            pltpu.VMEM((chunks, nsys, chunk_rows, dout), bf16),
            dma((chunks, n_run - 1)),
            dma((chunks, n_run - 1)),
            dma((n_run - 1,)),
            dma((n_run - 1,)),
            dma((n_rep - 1,)),
            dma((n_rep - 1,)),
            dma((2, chunks, n_x)),
            dma((2, chunks, n_x)),
            dma((2, chunks, n_x)),
            dma((2, chunks, n_x)),
            dma,
            dma((3,)),
            dma((4, chunks)),
        ],
        compiler_params=pltpu.CompilerParams(
            collective_id=0, has_side_effects=True, vmem_limit_bytes=56 * 1024 * 1024
        ),
        name="exchange_step",
    )(slots, meta, coef_out, merge_coef, weights, first_moment, second_moment)
    return (*outs[:3], outs[3][None])


def solution(mesh):
    placed = (
        P("rep", "run", None),
        P("rep", "run", None),
        P("rep", "run"),
        P("rep", "run"),
        P("rep", None, None),
        P("rep", "run", None),
        P("rep", "run", None),
        P("rep", "run", None),
    )
    return jax.shard_map(
        functools.partial(on_device, mesh.shape["run"], mesh.shape["rep"]),
        mesh=mesh,
        in_specs=placed,
        out_specs=(
            P("rep", "run", None),
            P("rep", "run", None),
            P("rep", "run", None),
            P("rep", None, "run", None),
        ),
        check_vma=False,
    )
```
